32 devices in a mesh: dp: 8 (over z, x), head: 4 (over y, core).
Axes of the slice: x: 2, y: 2, z: 4, core: 2. Of those that a mesh axis runs over, the one named last changes fastest.
Arguments:
- inputs: bfloat16 [8, 1024, 1152], P('dp', 'head'), may hold values from -6 to 6
- segments: int32 [8, 1024], P('dp'), may hold values from 0 to 7, never falling along the last dimension, each value on 1 to 512 neighbouring positions
- cotangent: bfloat16 [8, 1024, 1152], P('dp', 'head'), may hold values from -6 to 6
- query_weight: bfloat16 [1152, 1024], replicated, may hold values from -0.1875 to 0.1875
- key_weight: bfloat16 [1152, 256], replicated, may hold values from -0.1875 to 0.1875
- value_weight: bfloat16 [1152, 256], replicated, may hold values from -0.1875 to 0.1875
- out_weight: bfloat16 [1024, 1152], replicated, may hold values from -0.1875 to 0.1875
- gate_weight: bfloat16 [1152, 6912], P(None, 'head'), may hold values from -0.1875 to 0.1875
- up_weight: bfloat16 [1152, 6912], P(None, 'head'), may hold values from -0.1875 to 0.1875
- down_weight: bfloat16 [6912, 1152], P('head'), may hold values from -0.078125 to 0.078125
- input_gain: float32 [1152], replicated, may hold values from 0.1 to 1.9
- query_gain: float32 [256], replicated, may hold values from 0.1 to 1.9
- key_gain: float32 [256], replicated, may hold values from 0.1 to 1.9
- attn_gain: float32 [1152], replicated, may hold values from 0.1 to 1.9
- pre_ff_gain: float32 [1152], replicated, may hold values from 0.1 to 1.9
- post_ff_gain: float32 [1152], replicated, may hold values from 0.1 to 1.9
Outputs:
- layer_output: bfloat16 [8, 1024, 1152], P('dp', 'head')
- input_grad: float32 [8, 1024, 1152], P('dp', 'head')
- query_weight_grad: float32 [1152, 1024], replicated
- key_weight_grad: float32 [1152, 256], replicated
- value_weight_grad: float32 [1152, 256], replicated
- out_weight_grad: float32 [1024, 1152], replicated
- gate_weight_grad: float32 [1152, 6912], P('dp', 'head')
- up_weight_grad: float32 [1152, 6912], P('dp', 'head')
- down_weight_grad: float32 [6912, 1152], P('head', 'dp')
- input_gain_grad: float32 [1152], replicated
- query_gain_grad: float32 [256], replicated
- key_gain_grad: float32 [256], replicated
- attn_gain_grad: float32 [1152], replicated
- pre_ff_gain_grad: float32 [1152], replicated
- post_ff_gain_grad: float32 [1152], replicated
The draws below stay inside these ranges and needn't reach their ends.
Inputs may be any that keep to these rules, and one draw needn't show every extreme that they name: `segments`: within a row the document numbers never fall; each of the 8 documents has 1 to 512 tokens, and one has exactly 512.
All inputs are finite; a program needn't handle non-finite values.
Results may differ from the reference program's by a relative error of at most 0.02.
Values may be sent and summed in bfloat16 or wider, within the bound.
No kernel may reach another device: no remote copies, remote signals or barrier semaphores. Data moves between devices by JAX's collectives and lax.ppermute only.
A program may use at most 192 MiB of HBM per device.

```python
import math
import jax
import jax.numpy as jnp
import numpy as np
from jax import lax

D = 1152
QH = 4
HD = 256
FF = 6912
DOCS = 8
ROWS = 8
SEQ = 1024
QD = 1024
DOC_MOST = 512


def with_spikes(drawn, own_key, source, target, parts, factor):
    owner, partner = [(jnp.arange(drawn.shape[axis_at]) // (drawn.shape[axis_at] // parts)).reshape([-1 if axis == axis_at else 1 for axis in range(drawn.ndim)]) for axis_at in (source, target)]
    chosen = jax.random.permutation(own_key, parts)[partner]
    strong = (owner == chosen) | (owner == (partner + parts // 2) % parts)
    return jnp.where(strong, factor * drawn, drawn)


def shard_levels(stream_key, shape, cuts, smallest, largest):
    level = 1.0
    for axis_at, blocks in cuts:
        draws = jax.random.uniform(jax.random.fold_in(jax.random.fold_in(stream_key, 6), axis_at), (blocks,), jnp.float32, smallest / len(cuts), largest / len(cuts))
        level = level * jnp.repeat(jnp.exp(draws), shape[axis_at] // blocks).reshape((-1,) + (1,) * (len(shape) - 1 - axis_at))
    return level


def split_up(count, total, limit, slope):
    weights = [(1 << 20) // math.isqrt(standing ** slope) + 1 for standing in range(2, count + 1)]
    spare, given = total - limit - (count - 1), [1] * (count - 1)
    while spare > 0:
        free = [i for i in range(count - 1) if given[i] < limit]
        mass, budget = sum([weights[i] for i in free]), spare
        for i in free:
            more = min(limit - given[i], max(1, budget * weights[i] // mass), spare)
            given[i] = given[i] + more
            spare = spare - more
    return np.array([limit] + given)


def ragged(rng, number_of, total, bound, skew):
    if number_of == 2:
        one = jax.random.randint(rng, (), max(1, total - bound), min(bound, total - 1) + 1)
        return jnp.stack([one, total - one])
    tallies = jnp.asarray(split_up(number_of, total, bound, skew), jnp.int32)
    couples = (number_of - 1) // 2
    donor, taker = tallies[1:1 + 2 * couples:2], tallies[2:2 + 2 * couples:2]
    slack = jnp.minimum(donor - 1, bound - taker)
    shifted = jax.random.randint(jax.random.fold_in(rng, 1), (couples,), 0, 1 << 20) % (slack + 1)
    tallies = tallies.at[1:1 + 2 * couples:2].set(donor - shifted).at[2:2 + 2 * couples:2].set(taker + shifted)
    return tallies[jax.random.permutation(jax.random.fold_in(rng, 2), number_of)]


def centred(own_key, extent, width, bound, cuts=(), held_as=jnp.bfloat16):
    drawn = jax.random.normal(own_key, extent, jnp.float32) * width
    if len(cuts) > 0:
        drawn = shard_levels(own_key, extent, cuts, -0.22, 0.18) * drawn
    return jnp.clip(drawn, min=-bound, max=bound).astype(held_as)


def bell_draw_with(stream_key, shape, spread, most, split, heavy, kind=jnp.bfloat16):
    entries = spread * jax.random.normal(stream_key, shape, jnp.float32)
    if split:
        entries = entries * shard_levels(stream_key, shape, split, -0.22, 0.18)
    return jnp.clip(with_spikes(entries, jax.random.fold_in(stream_key, 3), *heavy), -most, most).astype(kind)


def setup_inputs(seed: int = 0) -> dict:
    arg_keys = jax.random.split(jax.random.key(seed), 17)
    return {
        "inputs": centred(arg_keys[0], (ROWS, SEQ, D), 1.0, 6.0, ((0, 8), (1, 4))),
        "segments": jax.vmap(lambda own: jnp.searchsorted(jnp.cumsum(ragged(own, DOCS, SEQ, DOC_MOST, 2)), jnp.arange(SEQ), side="right"))(jax.random.split(arg_keys[1], ROWS)).reshape((ROWS, SEQ)).astype(jnp.int32),
        "cotangent": bell_draw_with(arg_keys[2], (ROWS, SEQ, D), 1.0, 6.0, ((0, 8), (1, 4)), (0, 2, 8, 2.0)),
        "query_weight": centred(arg_keys[3], (D, QD), D ** -0.5, 0.1875),
        "key_weight": centred(arg_keys[4], (D, HD), D ** -0.5, 0.1875),
        "value_weight": centred(arg_keys[5], (D, HD), D ** -0.5, 0.1875),
        "out_weight": centred(arg_keys[6], (QD, D), QD ** -0.5, 0.1875),
        "gate_weight": centred(arg_keys[7], (D, FF), D ** -0.5, 0.1875, ((1, 4),)),
        "up_weight": centred(arg_keys[8], (D, FF), D ** -0.5, 0.1875, ((1, 4),)),
        "down_weight": centred(arg_keys[9], (FF, D), FF ** -0.5, 0.078125, ((0, 4),)),
        "input_gain": jnp.clip(1.0 + 0.18 * jax.random.normal(arg_keys[10], (D,), jnp.float32), 0.1, 1.9),
        "query_gain": jnp.clip(1.0 + 0.18 * jax.random.normal(arg_keys[11], (HD,), jnp.float32), 0.1, 1.9),
        "key_gain": jnp.clip(1.0 + 0.18 * jax.random.normal(arg_keys[12], (HD,), jnp.float32), 0.1, 1.9),
        "attn_gain": jnp.clip(1.0 + 0.18 * jax.random.normal(arg_keys[13], (D,), jnp.float32), 0.1, 1.9),
        "pre_ff_gain": jnp.clip(1.0 + 0.18 * jax.random.normal(arg_keys[14], (D,), jnp.float32), 0.1, 1.9),
        "post_ff_gain": jnp.clip(1.0 + 0.18 * jax.random.normal(arg_keys[15], (D,), jnp.float32), 0.1, 1.9),
    }


EPSILON = 1e-06
HIGHEST = lax.Precision.HIGHEST
ROPE_BASE = 1000000.0

@jax.custom_vjp
def low(v):
    return lax.optimization_barrier(v.astype(jnp.bfloat16)).astype(jnp.float32)

@jax.custom_vjp
def low_back(v):
    return v

def low_keep(v):
    return (low(v), None)

def low_pass(kept, grad):
    return (grad,)

def back_keep(v):
    return (v, None)

def back_low(kept, grad):
    return (low(grad),)
low.defvjp(low_keep, low_pass)
low_back.defvjp(back_keep, back_low)

def matmul(left, right):
    return jnp.dot(left, right, precision=HIGHEST, preferred_element_type=jnp.float32)

def rms_norm(values, gain):
    return values * lax.rsqrt(lax.optimization_barrier(jnp.mean(values * values, axis=-1, keepdims=True)) + EPSILON) * gain

def positions_of(segment_ids):
    count = segment_ids.shape[0]
    position_index = jnp.arange(count, dtype=jnp.int32)
    previous = jnp.concatenate([segment_ids[:1] - 1, segment_ids[:-1]])
    starts = jnp.where(segment_ids != previous, position_index, 0).astype(jnp.int32)
    return (position_index - lax.cummax(starts, axis=0)).astype(jnp.int32)

def rotary(values, positions, sign):
    half_width = values.shape[-1] // 2
    frequency = ROPE_BASE ** (-2.0 * jnp.arange(half_width, dtype=jnp.float32) / values.shape[-1])
    angle = positions.astype(jnp.float32)[:, None] * frequency[None, :]
    cosine_part = jnp.cos(angle)
    sine_part = jnp.sin(angle) * sign
    if values.ndim == 3:
        cosine_part = cosine_part[:, None, :]
        sine_part = sine_part[:, None, :]
    leading = values[..., :half_width]
    trailing = values[..., half_width:]
    return jnp.concatenate([leading * cosine_part - trailing * sine_part, trailing * cosine_part + leading * sine_part], axis=-1)

def layer_row(params, inputs_row, segment_ids):
    query_weight, key_weight, value_weight, out_weight, gate_weight, up_weight, down_weight, input_gain, query_gain, key_gain, attn_gain, pre_ff_gain, post_ff_gain = params
    positions = positions_of(segment_ids)
    normed = low(rms_norm(inputs_row, input_gain))
    q_proj = low_back(matmul(normed, query_weight)).reshape(SEQ, QH, HD)
    k_proj = low_back(matmul(normed, key_weight))
    v_proj = low_back(low(matmul(normed, value_weight)))
    query = low_back(low(rotary(rms_norm(q_proj, query_gain), positions, 1.0)))
    key = low_back(low(rotary(rms_norm(k_proj, key_gain), positions, 1.0)))
    raw_scores = jnp.einsum('qhd,kd->hqk', query, key, precision=HIGHEST, preferred_element_type=jnp.float32)
    scores = low_back(raw_scores * HD ** (-0.5))
    position_index = jnp.arange(SEQ, dtype=jnp.int32)
    allowed = (segment_ids[:, None] == segment_ids[None, :]) & (position_index[None, :] <= position_index[:, None])
    masked = jnp.where(allowed[None, :, :], scores, -1e+30)
    probabilities = low(jax.nn.softmax(masked, axis=-1))
    attended = jnp.einsum('hqk,kd->qhd', probabilities, v_proj, precision=HIGHEST, preferred_element_type=jnp.float32)
    attended = low_back(low(attended)).reshape(SEQ, QD)
    projected = low_back(matmul(attended, out_weight))
    after_attn = inputs_row + rms_norm(projected, attn_gain)
    pre_normed = low(rms_norm(after_attn, pre_ff_gain))
    gate_act = low_back(matmul(pre_normed, gate_weight))
    up_act = low_back(matmul(pre_normed, up_weight))
    hidden = low(jax.nn.gelu(gate_act, approximate=True) * up_act)
    ff_out = low_back(matmul(hidden, down_weight))
    return after_attn + rms_norm(ff_out, post_ff_gain)

def reference(inputs, segments, cotangent, query_weight, key_weight, value_weight, out_weight, gate_weight, up_weight, down_weight, input_gain, query_gain, key_gain, attn_gain, pre_ff_gain, post_ff_gain):
    params = tuple((item.astype(jnp.float32) for item in (query_weight, key_weight, value_weight, out_weight, gate_weight, up_weight, down_weight, input_gain, query_gain, key_gain, attn_gain, pre_ff_gain, post_ff_gain)))

    def one_row(totals, row_data):
        inputs_row, segment_ids, cot_row = row_data
        layer_out, pullback = jax.vjp(lambda weights, values: layer_row(weights, values, segment_ids), params, inputs_row.astype(jnp.float32))
        grads, input_row_grad = pullback(cot_row.astype(jnp.float32))
        totals = jax.tree.map(lambda total, grad: total + grad, totals, grads)
        return (totals, (layer_out.astype(jnp.bfloat16), input_row_grad))
    zeros = jax.tree.map(jnp.zeros_like, params)
    totals, (outputs, input_grads) = lax.scan(one_row, zeros, (inputs, segments, cotangent))
    return (outputs, input_grads, totals[0], totals[1], totals[2], totals[3], totals[4], totals[5], totals[6], totals[7], totals[8], totals[9], totals[10], totals[11], totals[12])
```

```python
from functools import partial

import jax
import jax.numpy as jnp
import numpy as np
from jax import lax
from jax.sharding import PartitionSpec as P

EPSILON = 1e-06
ROPE_BASE = 1000000.0
MASKED = -1e30
DOC_MOST = 512


def for_sending(x):
    return jax.tree.map(lambda a: a.astype(jnp.bfloat16) if a.dtype == jnp.float32 else a, x)


def rms_norm(values, gain):
    return values * lax.rsqrt(jnp.mean(values * values, axis=-1, keepdims=True) + EPSILON) * gain


def positions_of(segment_ids):
    count = segment_ids.shape[0]
    position_index = jnp.arange(count, dtype=jnp.int32)
    previous = jnp.concatenate([segment_ids[:1] - 1, segment_ids[:-1]])
    starts = jnp.where(segment_ids != previous, position_index, 0)
    return position_index - lax.cummax(starts, axis=0)


def rotary(values, positions, sign):
    half_width = values.shape[-1] // 2
    frequency = ROPE_BASE ** (-2.0 * jnp.arange(half_width, dtype=jnp.float32) / values.shape[-1])
    angle = positions.astype(jnp.float32)[:, None] * frequency[None, :]
    cosine_part = jnp.cos(angle)
    sine_part = jnp.sin(angle) * sign
    if values.ndim == 3:
        cosine_part = cosine_part[:, None, :]
        sine_part = sine_part[:, None, :]
    leading = values[..., :half_width]
    trailing = values[..., half_width:]
    return jnp.concatenate(
        [
            leading * cosine_part - trailing * sine_part,
            trailing * cosine_part + leading * sine_part,
        ],
        axis=-1,
    )


def product(left, right):
    return jnp.dot(left, right, preferred_element_type=jnp.float32)


def product_tn(left, right):
    return lax.dot_general(
        left, right, (((0,), (0,)), ((), ())), preferred_element_type=jnp.float32
    )


def product_nt(left, right):
    return lax.dot_general(
        left, right, (((1,), (1,)), ((), ())), preferred_element_type=jnp.float32
    )


def shards(
    inputs,
    segments,
    cotangent,
    query_weight,
    key_weight,
    value_weight,
    out_weight,
    gate_weight,
    up_weight,
    down_weight,
    input_gain,
    query_gain,
    key_gain,
    attn_gain,
    pre_ff_gain,
    post_ff_gain,
):
    low_type = jnp.bfloat16
    tok_rows = inputs.shape[1]
    head_dim = key_weight.shape[1]
    query_heads = query_weight.shape[1] // head_dim
    seq_len = segments.shape[1]
    score_scale = head_dim ** (-0.5)
    gelu_tanh = partial(jax.nn.gelu, approximate=True)
    x_rows = inputs[0].astype(jnp.float32)
    segment_ids = segments[0]
    all_positions = positions_of(segment_ids)
    own_start = lax.axis_index("head") * tok_rows
    positions = lax.dynamic_slice_in_dim(all_positions, own_start, tok_rows)
    normed, input_pull = jax.vjp(rms_norm, x_rows, input_gain)
    normed_low = normed.astype(low_type)
    q_proj = product(normed_low, query_weight).reshape(tok_rows, query_heads, head_dim)
    k_proj = product(normed_low, key_weight)
    v_low = product(normed_low, value_weight).astype(low_type)
    k_normed, key_pull = jax.vjp(rms_norm, k_proj, key_gain)
    k_low = rotary(k_normed, positions, 1.0).astype(low_type)
    kv_rows = lax.all_gather(
        jnp.concatenate([k_low, v_low], axis=1), "head", axis=0, tiled=True
    )
    q_normed, query_pull = jax.vjp(rms_norm, q_proj, query_gain)
    q_low = rotary(q_normed, positions, 1.0).astype(low_type)
    query_rows = jnp.concatenate([q_low[:, h, :] for h in range(query_heads)], axis=0)
    window = min(seq_len, tok_rows + DOC_MOST)
    window_start = jnp.maximum(own_start + tok_rows - window, 0)
    kv_window = lax.dynamic_slice_in_dim(kv_rows, window_start, window)
    key_rows = kv_window[:, :head_dim]
    value_rows = kv_window[:, head_dim:]
    own_segments = lax.dynamic_slice_in_dim(segment_ids, own_start, tok_rows)
    key_segments = lax.dynamic_slice_in_dim(segment_ids, window_start, window)
    own_index = own_start + jnp.arange(tok_rows, dtype=jnp.int32)
    key_index = window_start + jnp.arange(window, dtype=jnp.int32)
    allowed = (own_segments[:, None] == key_segments[None, :]) & (
        key_index[None, :] <= own_index[:, None]
    )
    raw_scores = product_nt(query_rows, key_rows) * score_scale
    masked = jnp.where(
        allowed[None], raw_scores.reshape(query_heads, tok_rows, window), MASKED
    ).reshape(query_heads * tok_rows, window)
    row_max = jnp.max(masked, axis=1, keepdims=True)
    exponent = jnp.exp(masked - row_max)
    row_total = jnp.sum(exponent, axis=1, keepdims=True)
    probabilities = exponent / row_total
    probs_low = probabilities.astype(low_type)
    attended_low = product(probs_low, value_rows).astype(low_type)
    mixed_rows = jnp.concatenate(
        [attended_low[h * tok_rows : (h + 1) * tok_rows] for h in range(query_heads)], axis=1
    )
    projected = product(mixed_rows, out_weight)
    attn_branch, attn_pull = jax.vjp(rms_norm, projected, attn_gain)
    after_attn = x_rows + attn_branch
    pre_normed, pre_pull = jax.vjp(rms_norm, after_attn, pre_ff_gain)
    rows_all = lax.all_gather(pre_normed.astype(low_type), "head", axis=0, tiled=True)
    gate_act = product(rows_all, gate_weight)
    up_act = product(rows_all, up_weight)
    gelu_gate, gelu_pull = jax.vjp(gelu_tanh, gate_act)
    hidden_low = (gelu_gate * up_act).astype(low_type)
    ff_out = lax.psum_scatter(
        product(
            lax.slice_in_dim(hidden_low, 0, tok_rows * lax.axis_size("head"), axis=0), down_weight
        ).astype(jnp.bfloat16),
        "head",
        scatter_dimension=0,
        tiled=True,
    ).astype(jnp.float32)
    post_branch, post_pull = jax.vjp(rms_norm, ff_out, post_ff_gain)
    layer_out = after_attn + post_branch
    out_grad = cotangent[0].astype(jnp.float32)
    ff_grad, post_gain_grad = post_pull(out_grad)
    ff_grad_all = lax.all_gather(for_sending(ff_grad.astype(low_type)), "head", axis=0, tiled=True)
    down_grad = product_tn(hidden_low, ff_grad_all)
    hidden_grad = product_nt(ff_grad_all, down_weight)
    up_grad_low = (hidden_grad * gelu_gate).astype(low_type)
    gate_grad_low = gelu_pull(hidden_grad * up_act)[0].astype(low_type)
    gate_grad = product_tn(rows_all, gate_grad_low)
    up_grad = product_tn(rows_all, up_grad_low)
    up_slice = lax.slice_in_dim(up_grad_low, 0, tok_rows * lax.axis_size("head"), axis=0)
    pre_grad = lax.psum_scatter(
        (product_nt(gate_grad_low, gate_weight) + product_nt(up_slice, up_weight)).astype(
            jnp.bfloat16
        ),
        "head",
        scatter_dimension=0,
        tiled=True,
    ).astype(jnp.float32)
    after_from_ff, pre_gain_grad = pre_pull(pre_grad)
    after_grad = out_grad + after_from_ff
    projected_grad, attn_gain_grad = attn_pull(after_grad)
    projected_low = projected_grad.astype(low_type)
    out_weight_grad = product_tn(mixed_rows, projected_low)
    mixed_grad = product_nt(projected_low, out_weight).astype(low_type)
    attended_grad = jnp.concatenate(
        [mixed_grad[:, h * head_dim : (h + 1) * head_dim] for h in range(query_heads)], axis=0
    )
    value_grad = product_tn(probs_low, attended_grad)
    prob_grad = product_nt(attended_grad, value_rows)
    row_delta = jnp.sum(prob_grad * probabilities, axis=1, keepdims=True)
    score_grad = (probabilities * (prob_grad - row_delta)).astype(low_type)
    query_grad_low = (product(score_grad, key_rows) * score_scale).astype(low_type)
    key_grad = product_tn(score_grad, query_rows) * score_scale
    kv_grad = lax.dynamic_update_slice_in_dim(
        jnp.zeros((seq_len, 2 * head_dim), low_type),
        jnp.concatenate([key_grad, value_grad], axis=1).astype(low_type),
        window_start,
        axis=0,
    )
    kv_share = lax.psum_scatter(kv_grad, "head", scatter_dimension=0, tiled=True).astype(
        jnp.float32
    )
    key_share = kv_share[:, :head_dim]
    value_share = kv_share[:, head_dim:]
    query_back = jnp.stack(
        [query_grad_low[h * tok_rows : (h + 1) * tok_rows] for h in range(query_heads)], axis=1
    )
    q_proj_grad, query_gain_grad = query_pull(
        rotary(query_back.astype(jnp.float32), positions, -1.0)
    )
    key_back = key_share.astype(low_type).astype(jnp.float32)
    k_proj_grad, key_gain_grad = key_pull(rotary(key_back, positions, -1.0))
    q_grad_low = q_proj_grad.reshape(tok_rows, query_heads * head_dim).astype(low_type)
    k_grad_low = k_proj_grad.astype(low_type)
    v_grad_low = value_share.astype(low_type)
    query_weight_grad = product_tn(normed_low, q_grad_low)
    key_weight_grad = product_tn(normed_low, k_grad_low)
    value_weight_grad = product_tn(normed_low, v_grad_low)
    normed_grad = (
        product_nt(q_grad_low, query_weight)
        + product_nt(k_grad_low, key_weight)
        + product_nt(v_grad_low, value_weight)
    )
    input_from_norm, input_gain_grad = input_pull(normed_grad)
    input_grad = after_grad + input_from_norm
    weight_grads = (query_weight_grad, key_weight_grad, value_weight_grad, out_weight_grad)
    gain_grads = (
        input_gain_grad,
        query_gain_grad,
        key_gain_grad,
        attn_gain_grad,
        pre_gain_grad,
        post_gain_grad,
    )
    gain_sums = lax.psum(jnp.concatenate(gain_grads), ("dp", "head"))
    gain_ends = np.cumsum([g.shape[0] for g in gain_grads])
    weight_sums = lax.psum(tuple(w.astype(low_type) for w in weight_grads), ("dp", "head"))
    summed = tuple(w.astype(jnp.float32) for w in weight_sums) + tuple(
        gain_sums[end - g.shape[0] : end] for g, end in zip(gain_grads, gain_ends)
    )
    gate_share, up_share, down_share = (
        lax.psum_scatter(
            gate_grad.astype(jnp.bfloat16), "dp", scatter_dimension=0, tiled=True
        ).astype(jnp.float32),
        lax.psum_scatter(
            up_grad.astype(jnp.bfloat16), "dp", scatter_dimension=0, tiled=True
        ).astype(jnp.float32),
        lax.psum_scatter(
            down_grad.astype(jnp.bfloat16), "dp", scatter_dimension=1, tiled=True
        ).astype(jnp.float32),
    )
    return (
        layer_out.astype(low_type)[None],
        input_grad[None],
        summed[0],
        summed[1],
        summed[2],
        summed[3],
        gate_share,
        up_share,
        down_share,
        summed[4],
        summed[5],
        summed[6],
        summed[7],
        summed[8],
        summed[9],
    )


def solution(mesh):
    in_specs = (
        P("dp", "head", None),
        P("dp", None),
        P("dp", "head", None),
        P(),
        P(),
        P(),
        P(),
        P(None, "head"),
        P(None, "head"),
        P("head", None),
        P(),
        P(),
        P(),
        P(),
        P(),
        P(),
    )
    out_specs = (
        P("dp", "head", None),
        P("dp", "head", None),
        P(),
        P(),
        P(),
        P(),
        P("dp", "head"),
        P("dp", "head"),
        P("head", "dp"),
        P(),
        P(),
        P(),
        P(),
        P(),
        P(),
    )
    return jax.shard_map(shards, mesh=mesh, in_specs=in_specs, out_specs=out_specs, check_vma=False)
```
